32 devices in a mesh: phys: 4 (over y, x), row: 2 (over core), col: 4 (over z).
Axes of the slice: x: 2, y: 2, z: 4, core: 2. Of those that a mesh axis runs over, the one named last changes fastest.
Arguments:
- rho_sites: bfloat16 [1, 16, 2048, 2048], P(None, 'phys', 'row', 'col'), may hold values from -0.0625 to 0.0625
- sigma_sites: bfloat16 [1, 16, 2048, 2048], P(None, 'phys', 'row', 'col'), may hold values from -0.0625 to 0.0625
- environment: float32 [2048, 2048], P('row', 'col'), may hold values from -6 to 6
Outputs:
- new_environment: float32 [2048, 2048], P('row', 'col')
The draws below stay inside these ranges and needn't reach their ends.
All inputs are finite; a program needn't handle non-finite values.
Results may differ from the reference program's by a relative error of at most 0.004.
Values may be sent and summed in bfloat16 or wider, within the bound.
A program may use at most 128 MiB of HBM per device.

```python
import jax
import jax.numpy as jnp

CHI = 2048
PAIRS = 16
SITES = 1


def shard_levels(own_key, shape, split, low, high):
    level = 1.0
    for position, shards_of in split:
        heights = jax.random.uniform(jax.random.fold_in(jax.random.fold_in(own_key, 6), position), (shards_of,), jnp.float32, low / len(split), high / len(split))
        level = level * jnp.repeat(jnp.exp(heights), shape[position] // shards_of).reshape((-1,) + (1,) * (len(shape) - 1 - position))
    return level


def bell_draw(key, shape, width, limit, split=(), dtype=jnp.bfloat16):
    values = width * jax.random.normal(key, shape, jnp.float32)
    if split:
        values = values * shard_levels(key, shape, split, -0.22, 0.18)
    return jnp.clip(values, -limit, limit).astype(dtype)


def setup_inputs(seed: int = 0) -> dict:
    key_of = jax.random.split(jax.random.key(seed), 4)
    rho_sites = bell_draw(key_of[0], (SITES, PAIRS, CHI, CHI), (4 * CHI) ** -0.5, 0.0625, ((1, 4), (2, 2), (3, 4)))
    sigma_sites = bell_draw(key_of[1], (SITES, PAIRS, CHI, CHI), (4 * CHI) ** -0.5, 0.0625, ((1, 4), (2, 2), (3, 4)))
    environment = bell_draw(key_of[2], (CHI, CHI), 1.0, 6.0, ((0, 2), (1, 4)), jnp.float32)
    return {"rho_sites": rho_sites, "sigma_sites": sigma_sites, "environment": environment}


def reference(rho_sites, sigma_sites, environment):
    env = environment
    for site in range(SITES):
        env_b = env.astype(jnp.bfloat16)
        total = jnp.zeros((CHI, CHI), jnp.float32)
        for pair in range(PAIRS):
            half = jnp.dot(env_b, sigma_sites[site, pair], preferred_element_type=jnp.float32).astype(jnp.bfloat16)
            total = total + jnp.dot(rho_sites[site, pair].T, half, preferred_element_type=jnp.float32)
        env = total
    return env
```

```python
import functools

import jax
import jax.numpy as jnp
from jax import lax
from jax.experimental import pallas as pl
from jax.experimental.pallas import tpu as pltpu
from jax.sharding import PartitionSpec as P

MESH = pl.DeviceIdType.MESH
NCH = 4
FROM_RIGHT = {
    0: [("r", 1, k) for k in range(4)] + [("r", 2, k) for k in range(4)],
    1: [("r", 2, 0), ("r", 2, 1), ("r", 3, 0), ("r", 3, 1), ("r", 2, 2), ("r", 3, 2), ("r", 2, 3), ("r", 3, 3)],
    2: [("r", 3, k) for k in range(4)] + [("h", p) for p in range(4)],
    3: [None] * 8,
}


def mirror(item):
    if item is None or item[0] == "h":
        return item
    return ("r", 3 - item[1], item[2])


FROM_LEFT = {3 - c: [mirror(i) for i in seq] for c, seq in FROM_RIGHT.items()}
PASS_LEFT = {
    (2, 1): [(3, 0)], (2, 2): [(3, 1), (2, 2)], (2, 3): [(3, 2), (2, 3)], (2, 4): [(3, 3)],
    (1, 1): [(2, 0)], (1, 2): [(2, 1)], (1, 5): [(2, 2)], (1, 7): [(2, 3)],
}
PASS_RIGHT = {(3 - c, t): [(3 - b, k) for b, k in v] for (c, t), v in PASS_LEFT.items()}
FIRST_LEFT = {1: [(1, k) for k in range(4)], 2: [(2, 0), (2, 1)], 3: [(3, k) for k in range(4)]}
FIRST_RIGHT = {3 - c: [(3 - b, k) for b, k in v] for c, v in FIRST_LEFT.items()}
F32 = jnp.float32
BF16 = jnp.bfloat16


def kernel(rho_ref, sig_ref, env_ref, out_ref,
           rho_g, sig, env_f, env_g, half, half_r, acc, psend, rbuf, s1, xbuf, s2, ybuf, fin,
           rl_send, rr_send, r_recv, h_send, h_recv, loc, sg_send, sg_recv,
           el_send, er_send, e_recv, ex_send, ex_recv, ey_send, ey_recv,
           row_send, row_recv, x_send, x_recv, y_send, y_recv, o_sem, z_send, z_recv):
    ph = lax.axis_index("phys")
    r = lax.axis_index("row")
    c = lax.axis_index("col")
    width = rho_g.shape[-1]
    rows = rho_g.shape[3]
    quarter = rows // 4
    ind3 = c // 3
    ind2 = c // 2 - ind3
    ind0 = (3 - c) // 3
    ind1 = 1 - ind0 - ind2 - ind3
    inds = (ind0, ind1, ind2, ind3)

    def pick(values):
        total = 0
        for i, v in zip(inds, values):
            total = total + i * v
        return total

    mate = {"row": 1 - r}
    xn = {"phys": ph + 1 - 2 * (ph % 2)}
    yn = {"phys": (ph + 2) % 4}
    left = {"col": c - 1}
    right = {"col": c + 1}

    def remote(src, dst, ss, rs, dev):
        return pltpu.make_async_remote_copy(src_ref=src, dst_ref=dst, send_sem=ss, recv_sem=rs,
                                            device_id=dev, device_id_type=MESH)

    load_env = pltpu.make_async_copy(env_ref, env_f, loc.at[0])
    load_env.start()
    load_rho = [pltpu.make_async_copy(rho_ref.at[0, :, :, pl.ds(k * width, width)], rho_g.at[c, k], loc.at[1 + k]) for k in range(NCH)]
    for cp in load_rho:
        cp.start()
    my_rows = pl.ds(pl.multiple_of(r * rows, rows), rows)
    load_sig = pltpu.make_async_copy(sig_ref.at[0], sig.at[:, my_rows, :], loc.at[1 + NCH])
    load_sig.start()

    barrier = pltpu.get_barrier_semaphore()
    for dev in (mate, xn, yn):
        pl.semaphore_signal(barrier, inc=1, device_id=dev, device_id_type=MESH)

    @pl.when(c > 0)
    def _():
        pl.semaphore_signal(barrier, inc=1, device_id=left, device_id_type=MESH)

    @pl.when(c < 3)
    def _():
        pl.semaphore_signal(barrier, inc=1, device_id=right, device_id_type=MESH)

    load_env.wait()
    env_g[c] = env_f[...].astype(BF16)
    pl.semaphore_wait(barrier, 3 + pick((1, 2, 2, 1)))

    q_rows = pl.ds(pl.multiple_of(ph * quarter, quarter), quarter)
    h_rows = pl.ds(pl.multiple_of((ph // 2) * 2 * quarter, 2 * quarter), 2 * quarter)

    def env_left(b):
        return remote(env_g.at[b, q_rows], env_g.at[b, q_rows], el_send.at[b], e_recv.at[b], left)

    def env_right(b):
        return remote(env_g.at[b, q_rows], env_g.at[b, q_rows], er_send.at[b], e_recv.at[b], right)

    def env_x(b):
        return remote(env_g.at[b, q_rows], env_g.at[b, q_rows], ex_send.at[b], ex_recv.at[b], xn)

    def env_y(b):
        return remote(env_g.at[b, h_rows], env_g.at[b, h_rows], ey_send.at[b], ey_recv.at[b], yn)

    def send_left(b, k):
        src = rho_g.at[b, k]
        return remote(src, rho_g.at[b, k], rl_send.at[b, k], r_recv.at[b, k], left)

    def send_right(b, k):
        src = rho_g.at[b, k]
        return remote(src, rho_g.at[b, k], rr_send.at[b, k], r_recv.at[b, k], right)

    @pl.when(c > 0)
    def _():
        env_left(c).start()

    @pl.when(c < 3)
    def _():
        env_right(c).start()

    give_sig = remote(sig_ref.at[0], sig.at[:, my_rows, :], sg_send, sg_recv, mate)
    give_sig.start()
    for cp in load_rho:
        cp.wait()

    def first_sends(cols_):
        for i in cols_:
            @pl.when(c == i)
            def _():
                for b, k in FIRST_LEFT.get(i, []):
                    send_left(b, k).start()
                for b, k in FIRST_RIGHT.get(i, []):
                    send_right(b, k).start()

    first_sends((0, 3))
    for d in range(1, 4):
        @pl.when(c >= d)
        def _(b=c - d):
            env_right(b).wait_recv()

            @pl.when(c < 3)
            def _():
                env_right(b).start()
            env_x(b).start()

        @pl.when(c + d <= 3)
        def _(b=c + d):
            env_left(b).wait_recv()

            @pl.when(c > 0)
            def _():
                env_left(b).start()
            env_x(b).start()
        if d == 2:
            first_sends((1, 2))

    def others(f):
        for d in range(1, 4):
            @pl.when(c >= d)
            def _(b=c - d):
                f(b)

            @pl.when(c + d <= 3)
            def _(b=c + d):
                f(b)

    def env_y_of(b):
        env_x(b).wait_recv()
        env_y(b).start()
    others(env_y_of)
    others(lambda b: env_y(b).wait_recv())
    load_sig.wait()
    give_sig.wait_recv()

    tile = min(256, rows)

    @pl.loop(0, 4)
    def _(p):
        @pl.loop(0, rows // tile)
        def _(m):
            here = pl.ds(pl.multiple_of(m * tile, tile), tile)
            total = jnp.dot(env_g[0, here, :], sig[p, pl.ds(0, 512), :], preferred_element_type=F32)
            for b in range(1, 4):
                total += jnp.dot(env_g[b, here, :], sig[p, pl.ds(b * 512, 512), :], preferred_element_type=F32)
            half[p, here, :] = total.astype(BF16)

    def unit_of(b, k):
        return (b % 2) * NCH + k

    def product(b, k, other, unit):
        acc[unit] = jnp.zeros_like(acc.at[unit])

        @pl.loop(0, 4)
        def _(p):
            acc[unit] += lax.dot_general(rho_g[b, k, p], other[p], (((0,), (0,)), ((), ())),
                                         preferred_element_type=F32)

    def row_copy(unit):
        return remote(psend.at[unit], rbuf.at[unit], row_send.at[unit], row_recv.at[unit], mate)

    def x_copy(unit):
        return remote(s1.at[unit], xbuf.at[unit], x_send.at[unit], x_recv.at[unit], xn)

    def y_copy(unit):
        return remote(s2.at[unit], ybuf.at[unit], y_send.at[unit], y_recv.at[unit], yn)

    def out_copy(unit):
        at = pl.ds(pl.multiple_of(unit * width, width), width)
        return pltpu.make_async_copy(fin.at[unit], out_ref.at[at], o_sem.at[unit])

    rem_b = pick((0, 3, 0, 0))
    mid = jnp.logical_and(c > 0, c < 3)

    def res_left(k):
        return remote(fin.at[2 * NCH + k], fin.at[NCH + k], z_send.at[k], z_recv.at[k], left)

    def res_right(k):
        return remote(fin.at[2 * NCH + k], fin.at[k], z_send.at[k], z_recv.at[k], right)

    def stage0(pos):
        valid, b, k, rem = pos

        @pl.when(valid)
        def _():
            unit = 2 * NCH + k if rem else unit_of(b, k)
            owner = b // 2
            own = 1 - (owner + r - 2 * owner * r)
            slot = own * unit + (1 - own) * (3 * NCH)
            product(b, k, half_r if rem else half, slot)

            @pl.when(b // 2 != r)
            def _():
                psend[unit] = acc[slot].astype(BF16)
                row_copy(unit).start()

    def owned(pos, f):
        valid, b, k, rem = pos

        @pl.when(jnp.logical_and(valid, b // 2 == r))
        def _():
            f(2 * NCH + k if rem else unit_of(b, k))

    def stage1(pos):
        def f(unit):
            row_copy(unit).wait_recv()
            s1[unit] = (acc[unit] + rbuf[unit].astype(F32)).astype(BF16)
            x_copy(unit).start()
        owned(pos, f)

    def stage2(pos):
        def f(unit):
            x_copy(unit).wait_recv()
            s2[unit] = (s1[unit].astype(F32) + xbuf[unit].astype(F32)).astype(BF16)
            y_copy(unit).start()
        owned(pos, f)

    def stage3(pos):
        def f(unit):
            y_copy(unit).wait_recv()
            fin[unit] = s2[unit].astype(F32) + ybuf[unit].astype(F32)
            if pos[3]:
                @pl.when(c == 1)
                def _():
                    res_left(pos[2]).start()

                @pl.when(c == 2)
                def _():
                    res_right(pos[2]).start()
            else:
                out_copy(unit).start()
        owned(pos, f)

    line = []

    def advance(pos):
        if pos is not None:
            stage0(pos)
        line.append(pos)
        n = len(line) - 1
        for lag, stage in ((2, stage1), (4, stage2), (6, stage3)):
            if n - lag >= 0 and line[n - lag] is not None:
                stage(line[n - lag])

    def half_copy(p, dev):
        return remote(half.at[p], half_r.at[p], h_send.at[p], h_recv.at[p], dev)

    true = c >= 0

    def arrive(t):
        for i in range(4):
            @pl.when(c == i)
            def _():
                for table, passed, send, wait in (
                    (FROM_RIGHT, PASS_LEFT, send_left, send_left),
                    (FROM_LEFT, PASS_RIGHT, send_right, send_right),
                ):
                    item = table[i][t - 1]
                    if item is None:
                        continue
                    if item[0] == "h":
                        half_copy(item[1], left if i == 2 else right).wait_recv()
                    else:
                        wait(item[1], item[2]).wait_recv()
                    for b, k in passed.get((i, t), []):
                        send(b, k).start()

    def positions(t):
        for table in (FROM_RIGHT, FROM_LEFT):
            items = [table[i][t - 1] for i in range(4)]
            ok = [1 if it is not None and it[0] == "r" else 0 for it in items]
            blocks = [it[1] if o else 0 for it, o in zip(items, ok)]
            chunks = [it[2] if o else 0 for it, o in zip(items, ok)]
            yield (pick(ok) == 1, pick(blocks), pick(chunks), False)

    arrive(1)
    for k in range(NCH):
        advance((true, c, k, False))

    @pl.when(c == 0)
    def _():
        for p in range(4):
            half_copy(p, right).start()

    @pl.when(c == 3)
    def _():
        for p in range(4):
            half_copy(p, left).start()
    for t in range(1, 9):
        if t > 1:
            arrive(t)
        for pos in positions(t):
            advance(pos)
    for k in range(NCH):
        advance((mid, rem_b, k, True))
    for _ in range(6):
        advance(None)

    @pl.when(jnp.logical_and(c == 0, r == 1))
    def _():
        for k in range(NCH):
            res_left(k).wait_recv()
            out_copy(NCH + k).start()

    @pl.when(jnp.logical_and(c == 3, r == 0))
    def _():
        for k in range(NCH):
            res_right(k).wait_recv()
            out_copy(k).start()

    for unit in range(2 * NCH):
        out_copy(unit).wait()
    give_sig.wait_send()

    @pl.when(c > 0)
    def _():
        env_left(c).wait_send()

    @pl.when(c < 3)
    def _():
        env_right(c).wait_send()
    for d in range(1, 4):
        @pl.when(c >= d)
        def _(b=c - d):
            @pl.when(c < 3)
            def _():
                env_right(b).wait_send()
            env_x(b).wait_send()
            env_y(b).wait_send()

        @pl.when(c + d <= 3)
        def _(b=c + d):
            @pl.when(c > 0)
            def _():
                env_left(b).wait_send()
            env_x(b).wait_send()
            env_y(b).wait_send()
    for i in range(4):
        @pl.when(c == i)
        def _():
            for first, passed, send in ((FIRST_LEFT, PASS_LEFT, send_left), (FIRST_RIGHT, PASS_RIGHT, send_right)):
                todo = list(first.get(i, []))
                for (j, t), v in passed.items():
                    if j == i:
                        todo += v
                for b, k in todo:
                    send(b, k).wait_send()
            if i in (0, 3):
                for p in range(4):
                    half_copy(p, right if i == 0 else left).wait_send()
    for pos in line:
        if pos is None:
            continue
        valid, b, k, rem = pos

        @pl.when(valid)
        def _():
            unit = 2 * NCH + k if rem else unit_of(b, k)

            @pl.when(b // 2 != r)
            def _():
                row_copy(unit).wait_send()

            @pl.when(b // 2 == r)
            def _():
                x_copy(unit).wait_send()
                y_copy(unit).wait_send()
                if rem:
                    @pl.when(c == 1)
                    def _():
                        res_left(k).wait_send()

                    @pl.when(c == 2)
                    def _():
                        res_right(k).wait_send()


def fused(rho_sites, sigma_sites, environment):
    _, pairs, rows, cols = rho_sites.shape
    width = cols // NCH
    units = 3 * NCH
    sem = pltpu.SemaphoreType.DMA
    piece = (units, width, cols)
    return pl.pallas_call(
        kernel,
        out_shape=jax.ShapeDtypeStruct(environment.shape, F32),
        in_specs=[pl.BlockSpec(memory_space=pl.ANY)] * 3,
        out_specs=pl.BlockSpec(memory_space=pl.ANY),
        scratch_shapes=[
            pltpu.VMEM((4, NCH, pairs, rows, width), BF16),
            pltpu.VMEM((pairs, 2 * rows, cols), BF16),
            pltpu.VMEM((rows, cols), F32),
            pltpu.VMEM((4, rows, cols), BF16),
            pltpu.VMEM((pairs, rows, cols), BF16),
            pltpu.VMEM((pairs, rows, cols), BF16),
            pltpu.VMEM((units + 1, width, cols), F32),
            pltpu.VMEM(piece, BF16), pltpu.VMEM(piece, BF16), pltpu.VMEM(piece, BF16),
            pltpu.VMEM(piece, BF16), pltpu.VMEM(piece, BF16), pltpu.VMEM(piece, BF16),
            pltpu.VMEM(piece, F32),
            sem((4, NCH)), sem((4, NCH)), sem((4, NCH)), sem((4,)), sem((4,)),
            sem((2 + NCH,)), sem, sem,
            sem((4,)), sem((4,)), sem((4,)), sem((4,)), sem((4,)), sem((4,)), sem((4,)),
            sem((units,)), sem((units,)), sem((units,)), sem((units,)), sem((units,)), sem((units,)),
            sem((units,)), sem((NCH,)), sem((NCH,)),
        ],
        compiler_params=pltpu.CompilerParams(
            collective_id=0, has_side_effects=True, vmem_limit_bytes=64 * 1024 * 1024 - 65536
        ),
    )(rho_sites, sigma_sites, environment)


def plain(rho_sites, sigma_sites, environment):
    env_whole = lax.all_gather(environment.astype(BF16), "col", axis=1, tiled=True)
    half = jnp.einsum(
        "ik,pkl->pil",
        env_whole,
        lax.all_gather(sigma_sites[0], "row", axis=1, tiled=True),
        preferred_element_type=F32,
    ).astype(BF16)
    partial_env = jnp.einsum(
        "pij,pil->jl",
        lax.all_gather(rho_sites[0], "col", axis=2, tiled=True),
        half,
        preferred_element_type=F32,
    )
    row_part = lax.psum_scatter(partial_env, "row", scatter_dimension=0, tiled=True)
    return lax.psum(row_part, "phys")


def solution(mesh):
    placed = (P(None, "phys", "row", "col"), P(None, "phys", "row", "col"), P("row", "col"))
    sizes = (mesh.shape["phys"], mesh.shape["row"], mesh.shape["col"])
    body = fused if sizes == (4, 2, 4) else plain
    return jax.shard_map(body, mesh=mesh, in_specs=placed, out_specs=P("row", "col"), check_vma=False)
```

```python
import functools

import jax
import jax.numpy as jnp
from jax import lax
from jax.experimental import pallas as pl
from jax.experimental.pallas import tpu as pltpu
from jax.sharding import PartitionSpec as P

MESH = pl.DeviceIdType.MESH
NCH = 4
FROM_RIGHT = {
    0: [("r", 1, k) for k in range(4)] + [("r", 2, k) for k in range(3)] + [None],
    1: [("r", 2, 0), ("r", 2, 1), ("r", 3, 0), ("r", 3, 1), ("r", 2, 2), ("r", 3, 2), ("r", 3, 3), ("r", 2, 3)],
    2: [("r", 3, k) for k in range(4)] + [("h", p) for p in range(4)],
    3: [None] * 8,
}


def mirror(item):
    if item is None or item[0] == "h":
        return item
    return ("r", 3 - item[1], item[2])


FROM_LEFT = {3 - c: [mirror(i) for i in seq] for c, seq in FROM_RIGHT.items()}
PASS_LEFT = {
    (2, 1): [(3, 0)], (2, 2): [(3, 1), (2, 2)], (2, 3): [(3, 2)], (2, 4): [(3, 3), (2, 3)],
    (1, 1): [(2, 0)], (1, 2): [(2, 1)], (1, 5): [(2, 2)],
}
PASS_RIGHT = {(3 - c, t): [(3 - b, k) for b, k in v] for (c, t), v in PASS_LEFT.items()}
FIRST_LEFT = {1: [(1, k) for k in range(4)], 2: [(2, 0), (2, 1)], 3: [(3, k) for k in range(4)]}
FIRST_RIGHT = {3 - c: [(3 - b, k) for b, k in v] for c, v in FIRST_LEFT.items()}
FOR_END = [(3, 0), (3, 1), (3, 2), (3, 3), (2, 3)]
NREM = len(FOR_END)
F32 = jnp.float32
BF16 = jnp.bfloat16


def kernel(rho_ref, sig_ref, env_ref, out_ref,
           rho_g, sig, env_f, env_g, half, half_r, acc, psend, rbuf, s1, xbuf, s2, ybuf, fin,
           rl_send, rr_send, r_recv, h_send, h_recv, loc, sg_send, sg_recv,
           el_send, er_send, e_recv, ex_send, ex_recv, ey_send, ey_recv,
           row_send, row_recv, x_send, x_recv, y_send, y_recv, o_sem, z_send, z_recv):
    ph = lax.axis_index("phys")
    r = lax.axis_index("row")
    c = lax.axis_index("col")
    width = rho_g.shape[-1]
    rows = rho_g.shape[3]
    quarter = rows // 4
    ind3 = c // 3
    ind2 = c // 2 - ind3
    ind0 = (3 - c) // 3
    ind1 = 1 - ind0 - ind2 - ind3
    inds = (ind0, ind1, ind2, ind3)

    def pick(values):
        total = 0
        for i, v in zip(inds, values):
            total = total + i * v
        return total

    mate = {"row": 1 - r}
    xn = {"phys": ph + 1 - 2 * (ph % 2)}
    yn = {"phys": (ph + 2) % 4}
    left = {"col": c - 1}
    right = {"col": c + 1}

    def remote(src, dst, ss, rs, dev):
        return pltpu.make_async_remote_copy(src_ref=src, dst_ref=dst, send_sem=ss, recv_sem=rs,
                                            device_id=dev, device_id_type=MESH)

    load_env = pltpu.make_async_copy(env_ref, env_f, loc.at[0])
    load_env.start()
    load_rho = [pltpu.make_async_copy(rho_ref.at[0, :, :, pl.ds(k * width, width)], rho_g.at[c, k], loc.at[1 + k]) for k in range(NCH)]
    for cp in load_rho:
        cp.start()
    my_rows = pl.ds(pl.multiple_of(r * rows, rows), rows)
    load_sig = pltpu.make_async_copy(sig_ref.at[0], sig.at[:, my_rows, :], loc.at[1 + NCH])
    load_sig.start()

    barrier = pltpu.get_barrier_semaphore()
    for dev in (mate, xn, yn):
        pl.semaphore_signal(barrier, inc=1, device_id=dev, device_id_type=MESH)

    @pl.when(c > 0)
    def _():
        pl.semaphore_signal(barrier, inc=1, device_id=left, device_id_type=MESH)

    @pl.when(c < 3)
    def _():
        pl.semaphore_signal(barrier, inc=1, device_id=right, device_id_type=MESH)

    load_env.wait()
    env_g[c] = env_f[...].astype(BF16)
    pl.semaphore_wait(barrier, 3 + pick((1, 2, 2, 1)))

    q_rows = pl.ds(pl.multiple_of(ph * quarter, quarter), quarter)
    h_rows = pl.ds(pl.multiple_of((ph // 2) * 2 * quarter, 2 * quarter), 2 * quarter)

    def env_left(b):
        return remote(env_g.at[b, q_rows], env_g.at[b, q_rows], el_send.at[b], e_recv.at[b], left)

    def env_right(b):
        return remote(env_g.at[b, q_rows], env_g.at[b, q_rows], er_send.at[b], e_recv.at[b], right)

    def env_x(b):
        return remote(env_g.at[b, q_rows], env_g.at[b, q_rows], ex_send.at[b], ex_recv.at[b], xn)

    def env_y(b):
        return remote(env_g.at[b, h_rows], env_g.at[b, h_rows], ey_send.at[b], ey_recv.at[b], yn)

    def send_left(b, k):
        src = rho_g.at[b, k]
        return remote(src, rho_g.at[b, k], rl_send.at[b, k], r_recv.at[b, k], left)

    def send_right(b, k):
        src = rho_g.at[b, k]
        return remote(src, rho_g.at[b, k], rr_send.at[b, k], r_recv.at[b, k], right)

    @pl.when(c > 0)
    def _():
        env_left(c).start()

    @pl.when(c < 3)
    def _():
        env_right(c).start()

    give_sig = remote(sig_ref.at[0], sig.at[:, my_rows, :], sg_send, sg_recv, mate)
    give_sig.start()
    for cp in load_rho:
        cp.wait()

    def first_sends(cols_):
        for i in cols_:
            @pl.when(c == i)
            def _():
                for b, k in FIRST_LEFT.get(i, []):
                    send_left(b, k).start()
                for b, k in FIRST_RIGHT.get(i, []):
                    send_right(b, k).start()

    first_sends(range(4))
    for d in range(1, 4):
        @pl.when(c >= d)
        def _(b=c - d):
            env_right(b).wait_recv()

            @pl.when(c < 3)
            def _():
                env_right(b).start()
            env_x(b).start()

        @pl.when(c + d <= 3)
        def _(b=c + d):
            env_left(b).wait_recv()

            @pl.when(c > 0)
            def _():
                env_left(b).start()
            env_x(b).start()

    def others(f):
        for d in range(1, 4):
            @pl.when(c >= d)
            def _(b=c - d):
                f(b)

            @pl.when(c + d <= 3)
            def _(b=c + d):
                f(b)

    def env_y_of(b):
        env_x(b).wait_recv()
        env_y(b).start()
    others(env_y_of)
    others(lambda b: env_y(b).wait_recv())
    load_sig.wait()
    give_sig.wait_recv()

    tile = min(256, rows)

    @pl.loop(0, 4)
    def _(p):
        @pl.loop(0, rows // tile)
        def _(m):
            here = pl.ds(pl.multiple_of(m * tile, tile), tile)
            total = jnp.dot(env_g[0, here, :], sig[p, pl.ds(0, 512), :], preferred_element_type=F32)
            for b in range(1, 4):
                total += jnp.dot(env_g[b, here, :], sig[p, pl.ds(b * 512, 512), :], preferred_element_type=F32)
            half[p, here, :] = total.astype(BF16)

    def unit_of(b, k):
        return (b % 2) * NCH + k

    def product(b, k, other, unit, first=0, last=4):
        if first == 0:
            acc[unit] = jnp.zeros_like(acc.at[unit])

        @pl.loop(first, last)
        def _(p):
            acc[unit] += lax.dot_general(rho_g[b, k, p], other[p], (((0,), (0,)), ((), ())),
                                         preferred_element_type=F32)

    def row_copy(unit):
        return remote(psend.at[unit], rbuf.at[unit], row_send.at[unit], row_recv.at[unit], mate)

    def x_copy(unit):
        return remote(s1.at[unit], xbuf.at[unit], x_send.at[unit], x_recv.at[unit], xn)

    def y_copy(unit):
        return remote(s2.at[unit], ybuf.at[unit], y_send.at[unit], y_recv.at[unit], yn)

    def out_copy(unit):
        at = pl.ds(pl.multiple_of(unit * width, width), width)
        return pltpu.make_async_copy(fin.at[unit], out_ref.at[at], o_sem.at[unit])

    mid = jnp.logical_and(c > 0, c < 3)

    def end_chunk(q):
        b, k = FOR_END[q]
        return pick((0, b, 3 - b, 0)), k

    def res_left(q):
        b, k = FOR_END[q]
        return remote(fin.at[2 * NCH + q], fin.at[(b % 2) * NCH + k], z_send.at[q], z_recv.at[q], left)

    def res_right(q):
        b, k = FOR_END[q]
        return remote(fin.at[2 * NCH + q], fin.at[((3 - b) % 2) * NCH + k], z_send.at[q], z_recv.at[q], right)

    def unit_at(pos):
        _, b, k, q = pos
        return unit_of(b, k) if q is None else 2 * NCH + q

    def slot_at(pos):
        _, b, k, q = pos
        if q is not None:
            return 2 * NCH + q
        owner = b // 2
        own = 1 - (owner + r - 2 * owner * r)
        return own * unit_of(b, k) + (1 - own) * (2 * NCH + NREM)

    def stage0(pos, first=0):
        valid, b, k, q = pos

        @pl.when(valid)
        def _():
            unit, slot = unit_at(pos), slot_at(pos)
            product(b, k, half if q is None else half_r, slot, first)

            @pl.when(b // 2 != r)
            def _():
                psend[unit] = acc[slot].astype(BF16)
                row_copy(unit).start()

    def owned(pos, f):
        valid, b, k, q = pos

        @pl.when(jnp.logical_and(valid, b // 2 == r))
        def _():
            f(unit_at(pos))

    def stage1(pos):
        def f(unit):
            row_copy(unit).wait_recv()
            s1[unit] = (acc[unit] + rbuf[unit].astype(F32)).astype(BF16)
            x_copy(unit).start()
        owned(pos, f)

    def stage2(pos):
        def f(unit):
            x_copy(unit).wait_recv()
            s2[unit] = (s1[unit].astype(F32) + xbuf[unit].astype(F32)).astype(BF16)
            y_copy(unit).start()
        owned(pos, f)

    def stage3(pos):
        def f(unit):
            y_copy(unit).wait_recv()
            fin[unit] = s2[unit].astype(F32) + ybuf[unit].astype(F32)
            if pos[3] is not None:
                @pl.when(c == 1)
                def _():
                    res_left(pos[3]).start()

                @pl.when(c == 2)
                def _():
                    res_right(pos[3]).start()
            else:
                out_copy(unit).start()
        owned(pos, f)

    line = []

    def advance(pos, first=0):
        if pos is not None:
            stage0(pos, first)
        line.append(pos)
        n = len(line) - 1
        for lag, stage in ((2, stage1), (4, stage2), (6, stage3)):
            if n - lag >= 0 and line[n - lag] is not None:
                stage(line[n - lag])

    def half_copy(p, dev):
        return remote(half.at[p], half_r.at[p], h_send.at[p], h_recv.at[p], dev)

    true = c >= 0

    def arrive(t, kinds="rh"):
        for i in range(4):
            @pl.when(c == i)
            def _():
                for table, passed, send in ((FROM_RIGHT, PASS_LEFT, send_left), (FROM_LEFT, PASS_RIGHT, send_right)):
                    item = table[i][t - 1]
                    if item is None or item[0] not in kinds:
                        continue
                    if item[0] == "h":
                        half_copy(item[1], left if i == 2 else right).wait_recv()
                    else:
                        send(item[1], item[2]).wait_recv()
                    for b, k in passed.get((i, t), []):
                        send(b, k).start()

    def positions(t):
        for table in (FROM_RIGHT, FROM_LEFT):
            items = [table[i][t - 1] for i in range(4)]
            ok = [1 if it is not None and it[0] == "r" else 0 for it in items]
            blocks = [it[1] if o else 0 for it, o in zip(items, ok)]
            chunks = [it[2] if o else 0 for it, o in zip(items, ok)]
            yield (pick(ok) == 1, pick(blocks), pick(chunks), None)

    def for_end(q):
        return (mid,) + end_chunk(q) + (q,)

    def part_for_end(q, first, last):
        @pl.when(mid)
        def _():
            product(*end_chunk(q), half_r, 2 * NCH + q, first, last)

    early = {5: [(0, 0, 1), (1, 0, 1)], 6: [(0, 1, 2), (1, 1, 2), (2, 0, 2)],
             7: [(0, 2, 3), (1, 2, 3), (2, 2, 3), (3, 0, 3)]}
    arrive(1)
    for k in range(NCH):
        advance((true, c, k, None))

    @pl.when(c == 0)
    def _():
        for p in range(4):
            half_copy(p, right).start()

    @pl.when(c == 3)
    def _():
        for p in range(4):
            half_copy(p, left).start()

    for t in range(1, 8):
        if t > 1:
            arrive(t)
        for pos in positions(t):
            advance(pos)
        for q, first, last in early.get(t, []):
            part_for_end(q, first, last)
    arrive(8, "h")
    for q in range(4):
        advance(for_end(q), 3)
    arrive(8, "r")
    advance(for_end(4))
    for pos in positions(8):
        advance(pos)
    for _ in range(6):
        advance(None)

    for i, keeper, got in ((0, 1, res_left), (3, 0, res_right)):
        @pl.when(jnp.logical_and(c == i, r == keeper))
        def _():
            for q in range(NREM):
                b, k = FOR_END[q]
                got(q).wait_recv()
                out_copy(unit_of(b if i == 0 else 3 - b, k)).start()

    for unit in range(2 * NCH):
        out_copy(unit).wait()
    give_sig.wait_send()

    @pl.when(c > 0)
    def _():
        env_left(c).wait_send()

    @pl.when(c < 3)
    def _():
        env_right(c).wait_send()
    for d in range(1, 4):
        @pl.when(c >= d)
        def _(b=c - d):
            @pl.when(c < 3)
            def _():
                env_right(b).wait_send()
            env_x(b).wait_send()
            env_y(b).wait_send()

        @pl.when(c + d <= 3)
        def _(b=c + d):
            @pl.when(c > 0)
            def _():
                env_left(b).wait_send()
            env_x(b).wait_send()
            env_y(b).wait_send()
    for i in range(4):
        @pl.when(c == i)
        def _():
            for first, passed, send in ((FIRST_LEFT, PASS_LEFT, send_left), (FIRST_RIGHT, PASS_RIGHT, send_right)):
                todo = list(first.get(i, []))
                for (j, t), v in passed.items():
                    if j == i:
                        todo += v
                for b, k in todo:
                    send(b, k).wait_send()
            if i in (0, 3):
                for p in range(4):
                    half_copy(p, right if i == 0 else left).wait_send()
    for pos in line:
        if pos is None:
            continue
        valid, b, k, q = pos

        @pl.when(valid)
        def _():
            unit = unit_at(pos)

            @pl.when(b // 2 != r)
            def _():
                row_copy(unit).wait_send()

            @pl.when(b // 2 == r)
            def _():
                x_copy(unit).wait_send()
                y_copy(unit).wait_send()
                if q is not None:
                    @pl.when(c == 1)
                    def _():
                        res_left(q).wait_send()

                    @pl.when(c == 2)
                    def _():
                        res_right(q).wait_send()


def fused(rho_sites, sigma_sites, environment):
    _, pairs, rows, cols = rho_sites.shape
    width = cols // NCH
    units = 2 * NCH + NREM
    sem = pltpu.SemaphoreType.DMA
    piece = (units, width, cols)
    return pl.pallas_call(
        kernel,
        out_shape=jax.ShapeDtypeStruct(environment.shape, F32),
        in_specs=[pl.BlockSpec(memory_space=pl.ANY)] * 3,
        out_specs=pl.BlockSpec(memory_space=pl.ANY),
        scratch_shapes=[
            pltpu.VMEM((4, NCH, pairs, rows, width), BF16),
            pltpu.VMEM((pairs, 2 * rows, cols), BF16),
            pltpu.VMEM((rows, cols), F32),
            pltpu.VMEM((4, rows, cols), BF16),
            pltpu.VMEM((pairs, rows, cols), BF16),
            pltpu.VMEM((pairs, rows, cols), BF16),
            pltpu.VMEM((units + 1, width, cols), F32),
            pltpu.VMEM(piece, BF16), pltpu.VMEM(piece, BF16), pltpu.VMEM(piece, BF16),
            pltpu.VMEM(piece, BF16), pltpu.VMEM(piece, BF16), pltpu.VMEM(piece, BF16),
            pltpu.VMEM(piece, F32),
            sem((4, NCH)), sem((4, NCH)), sem((4, NCH)), sem((4,)), sem((4,)),
            sem((2 + NCH,)), sem, sem,
            sem((4,)), sem((4,)), sem((4,)), sem((4,)), sem((4,)), sem((4,)), sem((4,)),
            sem((units,)), sem((units,)), sem((units,)), sem((units,)), sem((units,)), sem((units,)),
            sem((units,)), sem((NREM,)), sem((NREM,)),
        ],
        compiler_params=pltpu.CompilerParams(
            collective_id=0, has_side_effects=True, vmem_limit_bytes=64 * 1024 * 1024 - 65536
        ),
    )(rho_sites, sigma_sites, environment)


def plain(rho_sites, sigma_sites, environment):
    env_whole = lax.all_gather(environment.astype(BF16), "col", axis=1, tiled=True)
    half = jnp.einsum(
        "ik,pkl->pil",
        env_whole,
        lax.all_gather(sigma_sites[0], "row", axis=1, tiled=True),
        preferred_element_type=F32,
    ).astype(BF16)
    partial_env = jnp.einsum(
        "pij,pil->jl",
        lax.all_gather(rho_sites[0], "col", axis=2, tiled=True),
        half,
        preferred_element_type=F32,
    )
    row_part = lax.psum_scatter(partial_env, "row", scatter_dimension=0, tiled=True)
    return lax.psum(row_part, "phys")


def solution(mesh):
    placed = (P(None, "phys", "row", "col"), P(None, "phys", "row", "col"), P("row", "col"))
    sizes = (mesh.shape["phys"], mesh.shape["row"], mesh.shape["col"])
    body = fused if sizes == (4, 2, 4) else plain
    return jax.shard_map(body, mesh=mesh, in_specs=placed, out_specs=P("row", "col"), check_vma=False)
```

```python
import functools

import jax
import jax.numpy as jnp
from jax import lax
from jax.experimental import pallas as pl
from jax.experimental.pallas import tpu as pltpu
from jax.sharding import PartitionSpec as P

MESH = pl.DeviceIdType.MESH
NCH = 4
FROM_RIGHT = {
    0: [("r", 1, k) for k in range(4)] + [("r", 2, k) for k in range(3)] + [None],
    1: [("r", 2, 0), ("r", 2, 1), ("r", 3, 0), ("r", 3, 1), ("r", 2, 2), ("r", 3, 2), ("r", 3, 3), ("r", 2, 3)],
    2: [("r", 3, k) for k in range(4)] + [("h", p) for p in range(4)],
    3: [None] * 8,
}


def mirror(item):
    if item is None or item[0] == "h":
        return item
    return ("r", 3 - item[1], item[2])


FROM_LEFT = {3 - c: [mirror(i) for i in seq] for c, seq in FROM_RIGHT.items()}
PASS_LEFT = {
    (2, 1): [(3, 0)], (2, 2): [(3, 1), (2, 2)], (2, 3): [(3, 2)], (2, 4): [(3, 3), (2, 3)],
    (1, 1): [(2, 0)], (1, 2): [(2, 1)], (1, 5): [(2, 2)],
}
PASS_RIGHT = {(3 - c, t): [(3 - b, k) for b, k in v] for (c, t), v in PASS_LEFT.items()}
FIRST_LEFT = {1: [(1, k) for k in range(4)], 2: [(2, 0), (2, 1)], 3: [(3, k) for k in range(4)]}
FIRST_RIGHT = {3 - c: [(3 - b, k) for b, k in v] for c, v in FIRST_LEFT.items()}
FOR_END = [(3, 0), (3, 1), (3, 2), (3, 3), (2, 3)]
NREM = len(FOR_END)
F32 = jnp.float32
BF16 = jnp.bfloat16


def kernel(rho_ref, sig_ref, env_ref, out_ref,
           rho_g, sig, env_f, env_g, half, half_r, acc, psend, rbuf, s1, xbuf, s2, ybuf, fin,
           rl_send, rr_send, r_recv, h_send, h_recv, loc, sg_send, sg_recv,
           el_send, er_send, e_recv, ex_send, ex_recv, ey_send, ey_recv,
           row_send, row_recv, x_send, x_recv, y_send, y_recv, o_sem, z_send, z_recv):
    ph = lax.axis_index("phys")
    r = lax.axis_index("row")
    c = lax.axis_index("col")
    width = rho_g.shape[-1]
    rows = rho_g.shape[3]
    quarter = rows // 4
    ind3 = c // 3
    ind2 = c // 2 - ind3
    ind0 = (3 - c) // 3
    ind1 = 1 - ind0 - ind2 - ind3
    inds = (ind0, ind1, ind2, ind3)

    def pick(values):
        total = 0
        for i, v in zip(inds, values):
            total = total + i * v
        return total

    mate = {"row": 1 - r}
    xn = {"phys": ph + 1 - 2 * (ph % 2)}
    yn = {"phys": (ph + 2) % 4}
    left = {"col": c - 1}
    right = {"col": c + 1}

    def remote(src, dst, ss, rs, dev):
        return pltpu.make_async_remote_copy(src_ref=src, dst_ref=dst, send_sem=ss, recv_sem=rs,
                                            device_id=dev, device_id_type=MESH)

    load_env = pltpu.make_async_copy(env_ref, env_f, loc.at[0])
    load_env.start()
    load_rho = [pltpu.make_async_copy(rho_ref.at[0, :, :, pl.ds(k * width, width)], rho_g.at[c, k], loc.at[1 + k]) for k in range(NCH)]
    for cp in load_rho:
        cp.start()
    my_rows = pl.ds(pl.multiple_of(r * rows, rows), rows)
    load_sig = pltpu.make_async_copy(sig_ref.at[0], sig.at[:, my_rows, :], loc.at[1 + NCH])
    load_sig.start()

    barrier = pltpu.get_barrier_semaphore()
    for dev in (mate, xn, yn):
        pl.semaphore_signal(barrier, inc=1, device_id=dev, device_id_type=MESH)

    @pl.when(c > 0)
    def _():
        pl.semaphore_signal(barrier, inc=1, device_id=left, device_id_type=MESH)

    @pl.when(c < 3)
    def _():
        pl.semaphore_signal(barrier, inc=1, device_id=right, device_id_type=MESH)

    load_env.wait()
    env_g[c] = env_f[...].astype(BF16)
    pl.semaphore_wait(barrier, 3 + pick((1, 2, 2, 1)))

    q_rows = pl.ds(pl.multiple_of(ph * quarter, quarter), quarter)
    h_rows = pl.ds(pl.multiple_of((ph // 2) * 2 * quarter, 2 * quarter), 2 * quarter)

    def env_left(b):
        return remote(env_g.at[b, q_rows], env_g.at[b, q_rows], el_send.at[b], e_recv.at[b], left)

    def env_right(b):
        return remote(env_g.at[b, q_rows], env_g.at[b, q_rows], er_send.at[b], e_recv.at[b], right)

    def env_x(b):
        return remote(env_g.at[b, q_rows], env_g.at[b, q_rows], ex_send.at[b], ex_recv.at[b], xn)

    def env_y(b):
        return remote(env_g.at[b, h_rows], env_g.at[b, h_rows], ey_send.at[b], ey_recv.at[b], yn)

    def send_left(b, k):
        src = rho_g.at[b, k]
        return remote(src, rho_g.at[b, k], rl_send.at[b, k], r_recv.at[b, k], left)

    def send_right(b, k):
        src = rho_g.at[b, k]
        return remote(src, rho_g.at[b, k], rr_send.at[b, k], r_recv.at[b, k], right)

    @pl.when(c > 0)
    def _():
        env_left(c).start()

    @pl.when(c < 3)
    def _():
        env_right(c).start()

    give_sig = remote(sig_ref.at[0], sig.at[:, my_rows, :], sg_send, sg_recv, mate)
    give_sig.start()
    for cp in load_rho:
        cp.wait()

    def first_sends(cols_, first, last):
        for i in cols_:
            @pl.when(c == i)
            def _():
                for b, k in FIRST_LEFT.get(i, [])[first:last]:
                    send_left(b, k).start()
                for b, k in FIRST_RIGHT.get(i, [])[first:last]:
                    send_right(b, k).start()

    first_sends((0, 3), 0, 4)
    first_sends((1, 2), 0, 1)
    for d in range(1, 4):
        @pl.when(c >= d)
        def _(b=c - d):
            env_right(b).wait_recv()

            @pl.when(c < 3)
            def _():
                env_right(b).start()
            env_x(b).start()

        @pl.when(c + d <= 3)
        def _(b=c + d):
            env_left(b).wait_recv()

            @pl.when(c > 0)
            def _():
                env_left(b).start()
            env_x(b).start()
        if d == 2:
            first_sends((1, 2), 1, 4)

    def others(f):
        for d in range(1, 4):
            @pl.when(c >= d)
            def _(b=c - d):
                f(b)

            @pl.when(c + d <= 3)
            def _(b=c + d):
                f(b)

    def env_y_of(b):
        env_x(b).wait_recv()
        env_y(b).start()
    others(env_y_of)
    others(lambda b: env_y(b).wait_recv())
    load_sig.wait()
    give_sig.wait_recv()

    tile = min(256, rows)

    @pl.loop(0, 4)
    def _(p):
        @pl.loop(0, rows // tile)
        def _(m):
            here = pl.ds(pl.multiple_of(m * tile, tile), tile)
            total = jnp.dot(env_g[0, here, :], sig[p, pl.ds(0, 512), :], preferred_element_type=F32)
            for b in range(1, 4):
                total += jnp.dot(env_g[b, here, :], sig[p, pl.ds(b * 512, 512), :], preferred_element_type=F32)
            half[p, here, :] = total.astype(BF16)

    def unit_of(b, k):
        return (b % 2) * NCH + k

    def product(b, k, other, unit, first=0, last=4):
        if first == 0:
            acc[unit] = jnp.zeros_like(acc.at[unit])

        @pl.loop(first, last)
        def _(p):
            acc[unit] += lax.dot_general(rho_g[b, k, p], other[p], (((0,), (0,)), ((), ())),
                                         preferred_element_type=F32)

    def row_copy(unit):
        return remote(psend.at[unit], rbuf.at[unit], row_send.at[unit], row_recv.at[unit], mate)

    def x_copy(unit):
        return remote(s1.at[unit], xbuf.at[unit], x_send.at[unit], x_recv.at[unit], xn)

    def y_copy(unit):
        return remote(s2.at[unit], ybuf.at[unit], y_send.at[unit], y_recv.at[unit], yn)

    def out_copy(unit):
        at = pl.ds(pl.multiple_of(unit * width, width), width)
        return pltpu.make_async_copy(fin.at[unit], out_ref.at[at], o_sem.at[unit])

    mid = jnp.logical_and(c > 0, c < 3)

    def end_chunk(q):
        b, k = FOR_END[q]
        return pick((0, b, 3 - b, 0)), k

    def res_left(q):
        b, k = FOR_END[q]
        return remote(fin.at[2 * NCH + q], fin.at[(b % 2) * NCH + k], z_send.at[q], z_recv.at[q], left)

    def res_right(q):
        b, k = FOR_END[q]
        return remote(fin.at[2 * NCH + q], fin.at[((3 - b) % 2) * NCH + k], z_send.at[q], z_recv.at[q], right)

    def unit_at(pos):
        _, b, k, q = pos
        return unit_of(b, k) if q is None else 2 * NCH + q

    def slot_at(pos):
        _, b, k, q = pos
        if q is not None:
            return 2 * NCH + q
        owner = b // 2
        own = 1 - (owner + r - 2 * owner * r)
        return own * unit_of(b, k) + (1 - own) * (2 * NCH + NREM)

    def stage0(pos, first=0):
        valid, b, k, q = pos

        @pl.when(valid)
        def _():
            unit, slot = unit_at(pos), slot_at(pos)
            product(b, k, half if q is None else half_r, slot, first)

            @pl.when(b // 2 != r)
            def _():
                psend[unit] = acc[slot].astype(BF16)
                row_copy(unit).start()

    def owned(pos, f):
        valid, b, k, q = pos

        @pl.when(jnp.logical_and(valid, b // 2 == r))
        def _():
            f(unit_at(pos))

    def stage1(pos):
        def f(unit):
            row_copy(unit).wait_recv()
            s1[unit] = (acc[unit] + rbuf[unit].astype(F32)).astype(BF16)
            x_copy(unit).start()
        owned(pos, f)

    def stage2(pos):
        def f(unit):
            x_copy(unit).wait_recv()
            s2[unit] = (s1[unit].astype(F32) + xbuf[unit].astype(F32)).astype(BF16)
            y_copy(unit).start()
        owned(pos, f)

    def stage3(pos):
        def f(unit):
            y_copy(unit).wait_recv()
            fin[unit] = s2[unit].astype(F32) + ybuf[unit].astype(F32)
            if pos[3] is not None:
                @pl.when(c == 1)
                def _():
                    res_left(pos[3]).start()

                @pl.when(c == 2)
                def _():
                    res_right(pos[3]).start()
            else:
                out_copy(unit).start()
        owned(pos, f)

    line = []

    def advance(pos, first=0):
        if pos is not None:
            stage0(pos, first)
        line.append(pos)
        n = len(line) - 1
        for lag, stage in ((2, stage1), (4, stage2), (6, stage3)):
            if n - lag >= 0 and line[n - lag] is not None:
                stage(line[n - lag])

    def half_copy(p, dev):
        return remote(half.at[p], half_r.at[p], h_send.at[p], h_recv.at[p], dev)

    true = c >= 0

    def arrive(t, kinds="rh"):
        for i in range(4):
            @pl.when(c == i)
            def _():
                for table, passed, send in ((FROM_RIGHT, PASS_LEFT, send_left), (FROM_LEFT, PASS_RIGHT, send_right)):
                    item = table[i][t - 1]
                    if item is None or item[0] not in kinds:
                        continue
                    if item[0] == "h":
                        half_copy(item[1], left if i == 2 else right).wait_recv()
                    else:
                        send(item[1], item[2]).wait_recv()
                    for b, k in passed.get((i, t), []):
                        send(b, k).start()

    def positions(t):
        for table in (FROM_RIGHT, FROM_LEFT):
            items = [table[i][t - 1] for i in range(4)]
            ok = [1 if it is not None and it[0] == "r" else 0 for it in items]
            blocks = [it[1] if o else 0 for it, o in zip(items, ok)]
            chunks = [it[2] if o else 0 for it, o in zip(items, ok)]
            yield (pick(ok) == 1, pick(blocks), pick(chunks), None)

    def for_end(q):
        return (mid,) + end_chunk(q) + (q,)

    def part_for_end(q, first, last):
        @pl.when(mid)
        def _():
            product(*end_chunk(q), half_r, 2 * NCH + q, first, last)

    early = {5: [(0, 0, 1), (1, 0, 1)], 6: [(0, 1, 2), (1, 1, 2), (2, 0, 2)],
             7: [(0, 2, 3), (1, 2, 3), (2, 2, 3), (3, 0, 3)]}
    arrive(1)
    for k in range(NCH):
        advance((true, c, k, None))

    @pl.when(c == 0)
    def _():
        for p in range(4):
            half_copy(p, right).start()

    @pl.when(c == 3)
    def _():
        for p in range(4):
            half_copy(p, left).start()

    for t in range(1, 8):
        if t > 1:
            arrive(t)
        for pos in positions(t):
            advance(pos)
        for q, first, last in early.get(t, []):
            part_for_end(q, first, last)
    arrive(8, "h")
    for q in range(4):
        advance(for_end(q), 3)
    arrive(8, "r")
    advance(for_end(4))
    for pos in positions(8):
        advance(pos)
    for _ in range(6):
        advance(None)

    for i, keeper, got in ((0, 1, res_left), (3, 0, res_right)):
        @pl.when(jnp.logical_and(c == i, r == keeper))
        def _():
            for q in range(NREM):
                b, k = FOR_END[q]
                got(q).wait_recv()
                out_copy(unit_of(b if i == 0 else 3 - b, k)).start()

    for unit in range(2 * NCH):
        out_copy(unit).wait()
    give_sig.wait_send()

    @pl.when(c > 0)
    def _():
        env_left(c).wait_send()

    @pl.when(c < 3)
    def _():
        env_right(c).wait_send()
    for d in range(1, 4):
        @pl.when(c >= d)
        def _(b=c - d):
            @pl.when(c < 3)
            def _():
                env_right(b).wait_send()
            env_x(b).wait_send()
            env_y(b).wait_send()

        @pl.when(c + d <= 3)
        def _(b=c + d):
            @pl.when(c > 0)
            def _():
                env_left(b).wait_send()
            env_x(b).wait_send()
            env_y(b).wait_send()
    for i in range(4):
        @pl.when(c == i)
        def _():
            for first, passed, send in ((FIRST_LEFT, PASS_LEFT, send_left), (FIRST_RIGHT, PASS_RIGHT, send_right)):
                todo = list(first.get(i, []))
                for (j, t), v in passed.items():
                    if j == i:
                        todo += v
                for b, k in todo:
                    send(b, k).wait_send()
            if i in (0, 3):
                for p in range(4):
                    half_copy(p, right if i == 0 else left).wait_send()
    for pos in line:
        if pos is None:
            continue
        valid, b, k, q = pos

        @pl.when(valid)
        def _():
            unit = unit_at(pos)

            @pl.when(b // 2 != r)
            def _():
                row_copy(unit).wait_send()

            @pl.when(b // 2 == r)
            def _():
                x_copy(unit).wait_send()
                y_copy(unit).wait_send()
                if q is not None:
                    @pl.when(c == 1)
                    def _():
                        res_left(q).wait_send()

                    @pl.when(c == 2)
                    def _():
                        res_right(q).wait_send()


def fused(rho_sites, sigma_sites, environment):
    _, pairs, rows, cols = rho_sites.shape
    width = cols // NCH
    units = 2 * NCH + NREM
    sem = pltpu.SemaphoreType.DMA
    piece = (units, width, cols)
    return pl.pallas_call(
        kernel,
        out_shape=jax.ShapeDtypeStruct(environment.shape, F32),
        in_specs=[pl.BlockSpec(memory_space=pl.ANY)] * 3,
        out_specs=pl.BlockSpec(memory_space=pl.ANY),
        scratch_shapes=[
            pltpu.VMEM((4, NCH, pairs, rows, width), BF16),
            pltpu.VMEM((pairs, 2 * rows, cols), BF16),
            pltpu.VMEM((rows, cols), F32),
            pltpu.VMEM((4, rows, cols), BF16),
            pltpu.VMEM((pairs, rows, cols), BF16),
            pltpu.VMEM((pairs, rows, cols), BF16),
            pltpu.VMEM((units + 1, width, cols), F32),
            pltpu.VMEM(piece, BF16), pltpu.VMEM(piece, BF16), pltpu.VMEM(piece, BF16),
            pltpu.VMEM(piece, BF16), pltpu.VMEM(piece, BF16), pltpu.VMEM(piece, BF16),
            pltpu.VMEM(piece, F32),
            sem((4, NCH)), sem((4, NCH)), sem((4, NCH)), sem((4,)), sem((4,)),
            sem((2 + NCH,)), sem, sem,
            sem((4,)), sem((4,)), sem((4,)), sem((4,)), sem((4,)), sem((4,)), sem((4,)),
            sem((units,)), sem((units,)), sem((units,)), sem((units,)), sem((units,)), sem((units,)),
            sem((units,)), sem((NREM,)), sem((NREM,)),
        ],
        compiler_params=pltpu.CompilerParams(
            collective_id=0, has_side_effects=True, vmem_limit_bytes=64 * 1024 * 1024 - 65536
        ),
    )(rho_sites, sigma_sites, environment)


def plain(rho_sites, sigma_sites, environment):
    env_whole = lax.all_gather(environment.astype(BF16), "col", axis=1, tiled=True)
    half = jnp.einsum(
        "ik,pkl->pil",
        env_whole,
        lax.all_gather(sigma_sites[0], "row", axis=1, tiled=True),
        preferred_element_type=F32,
    ).astype(BF16)
    partial_env = jnp.einsum(
        "pij,pil->jl",
        lax.all_gather(rho_sites[0], "col", axis=2, tiled=True),
        half,
        preferred_element_type=F32,
    )
    row_part = lax.psum_scatter(partial_env, "row", scatter_dimension=0, tiled=True)
    return lax.psum(row_part, "phys")


def solution(mesh):
    placed = (P(None, "phys", "row", "col"), P(None, "phys", "row", "col"), P("row", "col"))
    sizes = (mesh.shape["phys"], mesh.shape["row"], mesh.shape["col"])
    body = fused if sizes == (4, 2, 4) else plain
    return jax.shard_map(body, mesh=mesh, in_specs=placed, out_specs=P("row", "col"), check_vma=False)
```

```python
import functools

import jax
import jax.numpy as jnp
from jax import lax
from jax.experimental import pallas as pl
from jax.experimental.pallas import tpu as pltpu
from jax.sharding import PartitionSpec as P

MESH = pl.DeviceIdType.MESH
NCH = 4
FROM_RIGHT = {
    0: [("r", 1, k) for k in range(4)] + [("r", 2, k) for k in range(3)] + [None],
    1: [("r", 2, 0), ("r", 2, 1), ("r", 3, 0), ("r", 3, 1), ("r", 2, 2), ("r", 3, 2), ("r", 3, 3), ("r", 2, 3)],
    2: [("r", 3, k) for k in range(4)] + [("h", p) for p in range(4)],
    3: [None] * 8,
}


def mirror(item):
    if item is None or item[0] == "h":
        return item
    return ("r", 3 - item[1], item[2])


FROM_LEFT = {3 - c: [mirror(i) for i in seq] for c, seq in FROM_RIGHT.items()}
PASS_LEFT = {
    (2, 1): [(3, 0)], (2, 2): [(3, 1), (2, 2)], (2, 3): [(3, 2)], (2, 4): [(3, 3), (2, 3)],
    (1, 1): [(2, 0)], (1, 2): [(2, 1)], (1, 5): [(2, 2)],
}
PASS_RIGHT = {(3 - c, t): [(3 - b, k) for b, k in v] for (c, t), v in PASS_LEFT.items()}
FIRST_LEFT = {1: [(1, k) for k in range(4)], 2: [(2, 0), (2, 1)], 3: [(3, k) for k in range(4)]}
FIRST_RIGHT = {3 - c: [(3 - b, k) for b, k in v] for c, v in FIRST_LEFT.items()}
FOR_END = [(3, 0), (3, 1), (3, 2), (3, 3), (2, 3)]
NREM = len(FOR_END)
F32 = jnp.float32
BF16 = jnp.bfloat16


def kernel(rho_ref, sig_ref, env_ref, out_ref,
           rho_g, sig, env_f, env_g, half, half_r, acc, psend, rbuf, s1, xbuf, s2, ybuf, fin,
           rl_send, rr_send, r_recv, h_send, h_recv, loc, sg_send, sg_recv,
           el_send, er_send, e_recv, ex_send, ex_recv, ey_send, ey_recv,
           row_send, row_recv, x_send, x_recv, y_send, y_recv, o_sem, z_send, z_recv):
    ph = lax.axis_index("phys")
    r = lax.axis_index("row")
    c = lax.axis_index("col")
    width = rho_g.shape[-1]
    rows = rho_g.shape[3]
    quarter = rows // 4
    ind3 = c // 3
    ind2 = c // 2 - ind3
    ind0 = (3 - c) // 3
    ind1 = 1 - ind0 - ind2 - ind3
    inds = (ind0, ind1, ind2, ind3)

    def pick(values):
        total = 0
        for i, v in zip(inds, values):
            total = total + i * v
        return total

    mate = {"row": 1 - r}
    xn = {"phys": ph + 1 - 2 * (ph % 2)}
    yn = {"phys": (ph + 2) % 4}
    left = {"col": c - 1}
    right = {"col": c + 1}

    def remote(src, dst, ss, rs, dev):
        return pltpu.make_async_remote_copy(src_ref=src, dst_ref=dst, send_sem=ss, recv_sem=rs,
                                            device_id=dev, device_id_type=MESH)

    load_env = pltpu.make_async_copy(env_ref, env_f, loc.at[0])
    load_env.start()
    load_rho = [pltpu.make_async_copy(rho_ref.at[0, :, :, pl.ds(k * width, width)], rho_g.at[c, k], loc.at[1 + k]) for k in range(NCH)]
    for cp in load_rho:
        cp.start()
    my_rows = pl.ds(pl.multiple_of(r * rows, rows), rows)
    load_sig = pltpu.make_async_copy(sig_ref.at[0], sig.at[:, my_rows, :], loc.at[1 + NCH])
    load_sig.start()

    barrier = pltpu.get_barrier_semaphore()
    for dev in (mate, xn, yn):
        pl.semaphore_signal(barrier, inc=1, device_id=dev, device_id_type=MESH)

    @pl.when(c > 0)
    def _():
        pl.semaphore_signal(barrier, inc=1, device_id=left, device_id_type=MESH)

    @pl.when(c < 3)
    def _():
        pl.semaphore_signal(barrier, inc=1, device_id=right, device_id_type=MESH)

    load_env.wait()
    env_g[c] = env_f[...].astype(BF16)
    pl.semaphore_wait(barrier, 3 + pick((1, 2, 2, 1)))

    q_rows = pl.ds(pl.multiple_of(ph * quarter, quarter), quarter)
    h_rows = pl.ds(pl.multiple_of((ph // 2) * 2 * quarter, 2 * quarter), 2 * quarter)

    def env_left(b):
        return remote(env_g.at[b, q_rows], env_g.at[b, q_rows], el_send.at[b], e_recv.at[b], left)

    def env_right(b):
        return remote(env_g.at[b, q_rows], env_g.at[b, q_rows], er_send.at[b], e_recv.at[b], right)

    def env_x(b):
        return remote(env_g.at[b, q_rows], env_g.at[b, q_rows], ex_send.at[b], ex_recv.at[b], xn)

    def env_y(b):
        return remote(env_g.at[b, h_rows], env_g.at[b, h_rows], ey_send.at[b], ey_recv.at[b], yn)

    def send_left(b, k):
        src = rho_g.at[b, k]
        return remote(src, rho_g.at[b, k], rl_send.at[b, k], r_recv.at[b, k], left)

    def send_right(b, k):
        src = rho_g.at[b, k]
        return remote(src, rho_g.at[b, k], rr_send.at[b, k], r_recv.at[b, k], right)

    @pl.when(c > 0)
    def _():
        env_left(c).start()

    @pl.when(c < 3)
    def _():
        env_right(c).start()

    give_sig = remote(sig_ref.at[0], sig.at[:, my_rows, :], sg_send, sg_recv, mate)
    give_sig.start()
    for cp in load_rho:
        cp.wait()

    def first_sends(cols_, first, last):
        for i in cols_:
            @pl.when(c == i)
            def _():
                for b, k in FIRST_LEFT.get(i, [])[first:last]:
                    send_left(b, k).start()
                for b, k in FIRST_RIGHT.get(i, [])[first:last]:
                    send_right(b, k).start()

    first_sends((0, 3), 0, 4)
    for d in range(1, 4):
        @pl.when(c >= d)
        def _(b=c - d):
            env_right(b).wait_recv()

            @pl.when(c < 3)
            def _():
                env_right(b).start()
            env_x(b).start()

        @pl.when(c + d <= 3)
        def _(b=c + d):
            env_left(b).wait_recv()

            @pl.when(c > 0)
            def _():
                env_left(b).start()
            env_x(b).start()
        if d == 2:
            first_sends((1, 2), 0, 4)

    def others(f):
        for d in range(1, 4):
            @pl.when(c >= d)
            def _(b=c - d):
                f(b)

            @pl.when(c + d <= 3)
            def _(b=c + d):
                f(b)

    def env_y_of(b):
        env_x(b).wait_recv()
        env_y(b).start()
    others(env_y_of)
    others(lambda b: env_y(b).wait_recv())
    load_sig.wait()
    give_sig.wait_recv()

    tile = min(256, rows)

    @pl.loop(0, 4)
    def _(p):
        @pl.loop(0, rows // tile)
        def _(m):
            here = pl.ds(pl.multiple_of(m * tile, tile), tile)
            total = jnp.dot(env_g[0, here, :], sig[p, pl.ds(0, 512), :], preferred_element_type=F32)
            for b in range(1, 4):
                total += jnp.dot(env_g[b, here, :], sig[p, pl.ds(b * 512, 512), :], preferred_element_type=F32)
            half[p, here, :] = total.astype(BF16)

    def unit_of(b, k):
        return (b % 2) * NCH + k

    def product(b, k, other, unit, first=0, last=4):
        if first == 0:
            acc[unit] = jnp.zeros_like(acc.at[unit])

        @pl.loop(first, last)
        def _(p):
            acc[unit] += lax.dot_general(rho_g[b, k, p], other[p], (((0,), (0,)), ((), ())),
                                         preferred_element_type=F32)

    def row_copy(unit):
        return remote(psend.at[unit], rbuf.at[unit], row_send.at[unit], row_recv.at[unit], mate)

    def x_copy(unit):
        return remote(s1.at[unit], xbuf.at[unit], x_send.at[unit], x_recv.at[unit], xn)

    def y_copy(unit):
        return remote(s2.at[unit], ybuf.at[unit], y_send.at[unit], y_recv.at[unit], yn)

    def out_copy(unit):
        at = pl.ds(pl.multiple_of(unit * width, width), width)
        return pltpu.make_async_copy(fin.at[unit], out_ref.at[at], o_sem.at[unit])

    mid = jnp.logical_and(c > 0, c < 3)

    def end_chunk(q):
        b, k = FOR_END[q]
        return pick((0, b, 3 - b, 0)), k

    def res_left(q):
        b, k = FOR_END[q]
        return remote(fin.at[2 * NCH + q], fin.at[(b % 2) * NCH + k], z_send.at[q], z_recv.at[q], left)

    def res_right(q):
        b, k = FOR_END[q]
        return remote(fin.at[2 * NCH + q], fin.at[((3 - b) % 2) * NCH + k], z_send.at[q], z_recv.at[q], right)

    def unit_at(pos):
        _, b, k, q = pos
        return unit_of(b, k) if q is None else 2 * NCH + q

    def slot_at(pos):
        _, b, k, q = pos
        if q is not None:
            return 2 * NCH + q
        owner = b // 2
        own = 1 - (owner + r - 2 * owner * r)
        return own * unit_of(b, k) + (1 - own) * (2 * NCH + NREM)

    def stage0(pos, first=0):
        valid, b, k, q = pos

        @pl.when(valid)
        def _():
            unit, slot = unit_at(pos), slot_at(pos)
            product(b, k, half if q is None else half_r, slot, first)

            @pl.when(b // 2 != r)
            def _():
                psend[unit] = acc[slot].astype(BF16)
                row_copy(unit).start()

    def owned(pos, f):
        valid, b, k, q = pos

        @pl.when(jnp.logical_and(valid, b // 2 == r))
        def _():
            f(unit_at(pos))

    def stage1(pos):
        def f(unit):
            row_copy(unit).wait_recv()
            s1[unit] = (acc[unit] + rbuf[unit].astype(F32)).astype(BF16)
            x_copy(unit).start()
        owned(pos, f)

    def stage2(pos):
        def f(unit):
            x_copy(unit).wait_recv()
            s2[unit] = (s1[unit].astype(F32) + xbuf[unit].astype(F32)).astype(BF16)
            y_copy(unit).start()
        owned(pos, f)

    def stage3(pos):
        def f(unit):
            y_copy(unit).wait_recv()
            fin[unit] = s2[unit].astype(F32) + ybuf[unit].astype(F32)
            if pos[3] is not None:
                @pl.when(c == 1)
                def _():
                    res_left(pos[3]).start()

                @pl.when(c == 2)
                def _():
                    res_right(pos[3]).start()
            else:
                out_copy(unit).start()
        owned(pos, f)

    line = []

    def advance(pos, first=0):
        if pos is not None:
            stage0(pos, first)
        line.append(pos)
        n = len(line) - 1
        for lag, stage in ((2, stage1), (4, stage2), (6, stage3)):
            if n - lag >= 0 and line[n - lag] is not None:
                stage(line[n - lag])

    def half_copy(p, dev):
        return remote(half.at[p], half_r.at[p], h_send.at[p], h_recv.at[p], dev)

    true = c >= 0

    def arrive(t, kinds="rh"):
        for i in range(4):
            @pl.when(c == i)
            def _():
                for table, passed, send in ((FROM_RIGHT, PASS_LEFT, send_left), (FROM_LEFT, PASS_RIGHT, send_right)):
                    item = table[i][t - 1]
                    if item is None or item[0] not in kinds:
                        continue
                    if item[0] == "h":
                        half_copy(item[1], left if i == 2 else right).wait_recv()
                    else:
                        send(item[1], item[2]).wait_recv()
                    for b, k in passed.get((i, t), []):
                        send(b, k).start()

    def positions(t):
        for table in (FROM_RIGHT, FROM_LEFT):
            items = [table[i][t - 1] for i in range(4)]
            ok = [1 if it is not None and it[0] == "r" else 0 for it in items]
            blocks = [it[1] if o else 0 for it, o in zip(items, ok)]
            chunks = [it[2] if o else 0 for it, o in zip(items, ok)]
            yield (pick(ok) == 1, pick(blocks), pick(chunks), None)

    def for_end(q):
        return (mid,) + end_chunk(q) + (q,)

    def part_for_end(q, first, last):
        @pl.when(mid)
        def _():
            product(*end_chunk(q), half_r, 2 * NCH + q, first, last)

    early = {5: [(0, 0, 1), (1, 0, 1)], 6: [(0, 1, 2), (1, 1, 2), (2, 0, 2)],
             7: [(0, 2, 3), (1, 2, 3), (2, 2, 3), (3, 0, 3)]}
    arrive(1)
    for k in range(NCH):
        advance((true, c, k, None))

    @pl.when(c == 0)
    def _():
        for p in range(4):
            half_copy(p, right).start()

    @pl.when(c == 3)
    def _():
        for p in range(4):
            half_copy(p, left).start()

    for t in range(1, 8):
        if t > 1:
            arrive(t)
        for pos in positions(t):
            advance(pos)
        for q, first, last in early.get(t, []):
            part_for_end(q, first, last)
    arrive(8, "h")
    for q in range(4):
        advance(for_end(q), 3)
    arrive(8, "r")
    advance(for_end(4))
    for pos in positions(8):
        advance(pos)
    for _ in range(6):
        advance(None)

    for i, keeper, got in ((0, 1, res_left), (3, 0, res_right)):
        @pl.when(jnp.logical_and(c == i, r == keeper))
        def _():
            for q in range(NREM):
                b, k = FOR_END[q]
                got(q).wait_recv()
                out_copy(unit_of(b if i == 0 else 3 - b, k)).start()

    for unit in range(2 * NCH):
        out_copy(unit).wait()
    give_sig.wait_send()

    @pl.when(c > 0)
    def _():
        env_left(c).wait_send()

    @pl.when(c < 3)
    def _():
        env_right(c).wait_send()
    for d in range(1, 4):
        @pl.when(c >= d)
        def _(b=c - d):
            @pl.when(c < 3)
            def _():
                env_right(b).wait_send()
            env_x(b).wait_send()
            env_y(b).wait_send()

        @pl.when(c + d <= 3)
        def _(b=c + d):
            @pl.when(c > 0)
            def _():
                env_left(b).wait_send()
            env_x(b).wait_send()
            env_y(b).wait_send()
    for i in range(4):
        @pl.when(c == i)
        def _():
            for first, passed, send in ((FIRST_LEFT, PASS_LEFT, send_left), (FIRST_RIGHT, PASS_RIGHT, send_right)):
                todo = list(first.get(i, []))
                for (j, t), v in passed.items():
                    if j == i:
                        todo += v
                for b, k in todo:
                    send(b, k).wait_send()
            if i in (0, 3):
                for p in range(4):
                    half_copy(p, right if i == 0 else left).wait_send()
    for pos in line:
        if pos is None:
            continue
        valid, b, k, q = pos

        @pl.when(valid)
        def _():
            unit = unit_at(pos)

            @pl.when(b // 2 != r)
            def _():
                row_copy(unit).wait_send()

            @pl.when(b // 2 == r)
            def _():
                x_copy(unit).wait_send()
                y_copy(unit).wait_send()
                if q is not None:
                    @pl.when(c == 1)
                    def _():
                        res_left(q).wait_send()

                    @pl.when(c == 2)
                    def _():
                        res_right(q).wait_send()


def fused(rho_sites, sigma_sites, environment):
    _, pairs, rows, cols = rho_sites.shape
    width = cols // NCH
    units = 2 * NCH + NREM
    sem = pltpu.SemaphoreType.DMA
    piece = (units, width, cols)
    return pl.pallas_call(
        kernel,
        out_shape=jax.ShapeDtypeStruct(environment.shape, F32),
        in_specs=[pl.BlockSpec(memory_space=pl.ANY)] * 3,
        out_specs=pl.BlockSpec(memory_space=pl.ANY),
        scratch_shapes=[
            pltpu.VMEM((4, NCH, pairs, rows, width), BF16),
            pltpu.VMEM((pairs, 2 * rows, cols), BF16),
            pltpu.VMEM((rows, cols), F32),
            pltpu.VMEM((4, rows, cols), BF16),
            pltpu.VMEM((pairs, rows, cols), BF16),
            pltpu.VMEM((pairs, rows, cols), BF16),
            pltpu.VMEM((units + 1, width, cols), F32),
            pltpu.VMEM(piece, BF16), pltpu.VMEM(piece, BF16), pltpu.VMEM(piece, BF16),
            pltpu.VMEM(piece, BF16), pltpu.VMEM(piece, BF16), pltpu.VMEM(piece, BF16),
            pltpu.VMEM(piece, F32),
            sem((4, NCH)), sem((4, NCH)), sem((4, NCH)), sem((4,)), sem((4,)),
            sem((2 + NCH,)), sem, sem,
            sem((4,)), sem((4,)), sem((4,)), sem((4,)), sem((4,)), sem((4,)), sem((4,)),
            sem((units,)), sem((units,)), sem((units,)), sem((units,)), sem((units,)), sem((units,)),
            sem((units,)), sem((NREM,)), sem((NREM,)),
        ],
        compiler_params=pltpu.CompilerParams(
            collective_id=0, has_side_effects=True, vmem_limit_bytes=64 * 1024 * 1024 - 65536
        ),
    )(rho_sites, sigma_sites, environment)


def plain(rho_sites, sigma_sites, environment):
    env_whole = lax.all_gather(environment.astype(BF16), "col", axis=1, tiled=True)
    half = jnp.einsum(
        "ik,pkl->pil",
        env_whole,
        lax.all_gather(sigma_sites[0], "row", axis=1, tiled=True),
        preferred_element_type=F32,
    ).astype(BF16)
    partial_env = jnp.einsum(
        "pij,pil->jl",
        lax.all_gather(rho_sites[0], "col", axis=2, tiled=True),
        half,
        preferred_element_type=F32,
    )
    row_part = lax.psum_scatter(partial_env, "row", scatter_dimension=0, tiled=True)
    return lax.psum(row_part, "phys")


def solution(mesh):
    placed = (P(None, "phys", "row", "col"), P(None, "phys", "row", "col"), P("row", "col"))
    sizes = (mesh.shape["phys"], mesh.shape["row"], mesh.shape["col"])
    body = fused if sizes == (4, 2, 4) else plain
    return jax.shard_map(body, mesh=mesh, in_specs=placed, out_specs=P("row", "col"), check_vma=False)
```

```python
import functools

import jax
import jax.numpy as jnp
from jax import lax
from jax.experimental import pallas as pl
from jax.experimental.pallas import tpu as pltpu
from jax.sharding import PartitionSpec as P

MESH = pl.DeviceIdType.MESH
NCH = 4
FROM_RIGHT = {
    0: [("r", 1, k) for k in range(4)] + [("r", 2, k) for k in range(3)] + [None],
    1: [("r", 2, 0), ("r", 2, 1), ("r", 2, 2), ("r", 3, 0), ("r", 3, 1), ("r", 3, 2), ("r", 3, 3), ("r", 2, 3)],
    2: [("r", 3, k) for k in range(4)] + [("h", p) for p in range(4)],
    3: [None] * 8,
}


def mirror(item):
    if item is None or item[0] == "h":
        return item
    return ("r", 3 - item[1], item[2])


FROM_LEFT = {3 - c: [mirror(i) for i in seq] for c, seq in FROM_RIGHT.items()}
PASS_LEFT = {
    (2, 1): [(3, 0)], (2, 2): [(3, 1)], (2, 3): [(3, 2)], (2, 4): [(3, 3), (2, 3)],
    (1, 1): [(2, 0)], (1, 2): [(2, 1)], (1, 3): [(2, 2)],
}
PASS_RIGHT = {(3 - c, t): [(3 - b, k) for b, k in v] for (c, t), v in PASS_LEFT.items()}
FIRST_LEFT = {1: [(1, k) for k in range(4)], 2: [(2, 0), (2, 1), (2, 2)], 3: [(3, k) for k in range(4)]}
FIRST_RIGHT = {3 - c: [(3 - b, k) for b, k in v] for c, v in FIRST_LEFT.items()}
FOR_END = [(3, 0), (3, 1), (3, 2), (3, 3), (2, 3)]
NREM = len(FOR_END)
F32 = jnp.float32
BF16 = jnp.bfloat16


def kernel(rho_ref, sig_ref, env_ref, out_ref,
           rho_g, sig, env_f, env_g, half, half_r, acc, psend, rbuf, s1, xbuf, s2, ybuf, fin,
           rl_send, rr_send, r_recv, h_send, h_recv, loc, sg_send, sg_recv,
           el_send, er_send, e_recv, ex_send, ex_recv, ey_send, ey_recv,
           row_send, row_recv, x_send, x_recv, y_send, y_recv, o_sem, z_send, z_recv):
    ph = lax.axis_index("phys")
    r = lax.axis_index("row")
    c = lax.axis_index("col")
    width = rho_g.shape[-1]
    rows = rho_g.shape[3]
    quarter = rows // 4
    ind3 = c // 3
    ind2 = c // 2 - ind3
    ind0 = (3 - c) // 3
    ind1 = 1 - ind0 - ind2 - ind3
    inds = (ind0, ind1, ind2, ind3)

    def pick(values):
        total = 0
        for i, v in zip(inds, values):
            total = total + i * v
        return total

    mate = {"row": 1 - r}
    xn = {"phys": ph + 1 - 2 * (ph % 2)}
    yn = {"phys": (ph + 2) % 4}
    left = {"col": c - 1}
    right = {"col": c + 1}

    def remote(src, dst, ss, rs, dev):
        return pltpu.make_async_remote_copy(src_ref=src, dst_ref=dst, send_sem=ss, recv_sem=rs,
                                            device_id=dev, device_id_type=MESH)

    load_env = pltpu.make_async_copy(env_ref, env_f, loc.at[0])
    load_env.start()
    load_rho = [pltpu.make_async_copy(rho_ref.at[0, :, :, pl.ds(k * width, width)], rho_g.at[c, k], loc.at[1 + k]) for k in range(NCH)]
    for cp in load_rho:
        cp.start()
    my_rows = pl.ds(pl.multiple_of(r * rows, rows), rows)
    load_sig = pltpu.make_async_copy(sig_ref.at[0], sig.at[:, my_rows, :], loc.at[1 + NCH])
    load_sig.start()

    barrier = pltpu.get_barrier_semaphore()
    for dev in (mate, xn, yn):
        pl.semaphore_signal(barrier, inc=1, device_id=dev, device_id_type=MESH)

    @pl.when(c > 0)
    def _():
        pl.semaphore_signal(barrier, inc=1, device_id=left, device_id_type=MESH)

    @pl.when(c < 3)
    def _():
        pl.semaphore_signal(barrier, inc=1, device_id=right, device_id_type=MESH)

    load_env.wait()
    env_g[c] = env_f[...].astype(BF16)
    pl.semaphore_wait(barrier, 3 + pick((1, 2, 2, 1)))

    q_rows = pl.ds(pl.multiple_of(ph * quarter, quarter), quarter)
    h_rows = pl.ds(pl.multiple_of((ph // 2) * 2 * quarter, 2 * quarter), 2 * quarter)

    def env_left(b):
        return remote(env_g.at[b, q_rows], env_g.at[b, q_rows], el_send.at[b], e_recv.at[b], left)

    def env_right(b):
        return remote(env_g.at[b, q_rows], env_g.at[b, q_rows], er_send.at[b], e_recv.at[b], right)

    def env_x(b):
        return remote(env_g.at[b, q_rows], env_g.at[b, q_rows], ex_send.at[b], ex_recv.at[b], xn)

    def env_y(b):
        return remote(env_g.at[b, h_rows], env_g.at[b, h_rows], ey_send.at[b], ey_recv.at[b], yn)

    def send_left(b, k):
        src = rho_g.at[b, k]
        return remote(src, rho_g.at[b, k], rl_send.at[b, k], r_recv.at[b, k], left)

    def send_right(b, k):
        src = rho_g.at[b, k]
        return remote(src, rho_g.at[b, k], rr_send.at[b, k], r_recv.at[b, k], right)

    @pl.when(c > 0)
    def _():
        env_left(c).start()

    @pl.when(c < 3)
    def _():
        env_right(c).start()

    give_sig = remote(sig_ref.at[0], sig.at[:, my_rows, :], sg_send, sg_recv, mate)
    give_sig.start()
    for cp in load_rho:
        cp.wait()

    def first_sends(cols_, first, last):
        for i in cols_:
            @pl.when(c == i)
            def _():
                for b, k in FIRST_LEFT.get(i, [])[first:last]:
                    send_left(b, k).start()
                for b, k in FIRST_RIGHT.get(i, [])[first:last]:
                    send_right(b, k).start()

    first_sends((0, 3), 0, 4)
    for d in range(1, 4):
        @pl.when(c >= d)
        def _(b=c - d):
            env_right(b).wait_recv()

            @pl.when(c < 3)
            def _():
                env_right(b).start()
            env_x(b).start()

        @pl.when(c + d <= 3)
        def _(b=c + d):
            env_left(b).wait_recv()

            @pl.when(c > 0)
            def _():
                env_left(b).start()
            env_x(b).start()
        if d == 2:
            first_sends((1, 2), 0, 4)

    def others(f):
        for d in range(1, 4):
            @pl.when(c >= d)
            def _(b=c - d):
                f(b)

            @pl.when(c + d <= 3)
            def _(b=c + d):
                f(b)

    def env_y_of(b):
        env_x(b).wait_recv()
        env_y(b).start()
    others(env_y_of)
    others(lambda b: env_y(b).wait_recv())
    load_sig.wait()
    give_sig.wait_recv()

    tile = min(256, rows)

    @pl.loop(0, 4)
    def _(p):
        @pl.loop(0, rows // tile)
        def _(m):
            here = pl.ds(pl.multiple_of(m * tile, tile), tile)
            total = jnp.dot(env_g[0, here, :], sig[p, pl.ds(0, 512), :], preferred_element_type=F32)
            for b in range(1, 4):
                total += jnp.dot(env_g[b, here, :], sig[p, pl.ds(b * 512, 512), :], preferred_element_type=F32)
            half[p, here, :] = total.astype(BF16)

    def unit_of(b, k):
        return (b % 2) * NCH + k

    def product(b, k, other, unit, first=0, last=4):
        if first == 0:
            acc[unit] = jnp.zeros_like(acc.at[unit])

        @pl.loop(first, last)
        def _(p):
            acc[unit] += lax.dot_general(rho_g[b, k, p], other[p], (((0,), (0,)), ((), ())),
                                         preferred_element_type=F32)

    def row_copy(unit):
        return remote(psend.at[unit], rbuf.at[unit], row_send.at[unit], row_recv.at[unit], mate)

    def x_copy(unit):
        return remote(s1.at[unit], xbuf.at[unit], x_send.at[unit], x_recv.at[unit], xn)

    def y_copy(unit):
        return remote(s2.at[unit], ybuf.at[unit], y_send.at[unit], y_recv.at[unit], yn)

    def out_copy(unit):
        at = pl.ds(pl.multiple_of(unit * width, width), width)
        return pltpu.make_async_copy(fin.at[unit], out_ref.at[at], o_sem.at[unit])

    mid = jnp.logical_and(c > 0, c < 3)

    def end_chunk(q):
        b, k = FOR_END[q]
        return pick((0, b, 3 - b, 0)), k

    def res_left(q):
        b, k = FOR_END[q]
        return remote(fin.at[2 * NCH + q], fin.at[(b % 2) * NCH + k], z_send.at[q], z_recv.at[q], left)

    def res_right(q):
        b, k = FOR_END[q]
        return remote(fin.at[2 * NCH + q], fin.at[((3 - b) % 2) * NCH + k], z_send.at[q], z_recv.at[q], right)

    def unit_at(pos):
        _, b, k, q = pos
        return unit_of(b, k) if q is None else 2 * NCH + q

    def slot_at(pos):
        _, b, k, q = pos
        if q is not None:
            return 2 * NCH + q
        owner = b // 2
        own = 1 - (owner + r - 2 * owner * r)
        return own * unit_of(b, k) + (1 - own) * (2 * NCH + NREM)

    def stage0(pos, first=0):
        valid, b, k, q = pos

        @pl.when(valid)
        def _():
            unit, slot = unit_at(pos), slot_at(pos)
            product(b, k, half if q is None else half_r, slot, first)

            @pl.when(b // 2 != r)
            def _():
                psend[unit] = acc[slot].astype(BF16)
                row_copy(unit).start()

    def owned(pos, f):
        valid, b, k, q = pos

        @pl.when(jnp.logical_and(valid, b // 2 == r))
        def _():
            f(unit_at(pos))

    def stage1(pos):
        def f(unit):
            row_copy(unit).wait_recv()
            s1[unit] = (acc[unit] + rbuf[unit].astype(F32)).astype(BF16)
            x_copy(unit).start()
        owned(pos, f)

    def stage2(pos):
        def f(unit):
            x_copy(unit).wait_recv()
            s2[unit] = (s1[unit].astype(F32) + xbuf[unit].astype(F32)).astype(BF16)
            y_copy(unit).start()
        owned(pos, f)

    def stage3(pos):
        def f(unit):
            y_copy(unit).wait_recv()
            fin[unit] = s2[unit].astype(F32) + ybuf[unit].astype(F32)
            if pos[3] is not None:
                @pl.when(c == 1)
                def _():
                    res_left(pos[3]).start()

                @pl.when(c == 2)
                def _():
                    res_right(pos[3]).start()
            else:
                out_copy(unit).start()
        owned(pos, f)

    line = []

    def advance(pos, first=0):
        if pos is not None:
            stage0(pos, first)
        line.append(pos)
        n = len(line) - 1
        for lag, stage in ((2, stage1), (4, stage2), (6, stage3)):
            if n - lag >= 0 and line[n - lag] is not None:
                stage(line[n - lag])

    def half_copy(p, dev):
        return remote(half.at[p], half_r.at[p], h_send.at[p], h_recv.at[p], dev)

    true = c >= 0

    def arrive(t, kinds="rh"):
        for i in range(4):
            @pl.when(c == i)
            def _():
                for table, passed, send in ((FROM_RIGHT, PASS_LEFT, send_left), (FROM_LEFT, PASS_RIGHT, send_right)):
                    item = table[i][t - 1]
                    if item is None or item[0] not in kinds:
                        continue
                    if item[0] == "h":
                        half_copy(item[1], left if i == 2 else right).wait_recv()
                    else:
                        send(item[1], item[2]).wait_recv()
                    for b, k in passed.get((i, t), []):
                        send(b, k).start()

    def positions(t):
        for table in (FROM_RIGHT, FROM_LEFT):
            items = [table[i][t - 1] for i in range(4)]
            ok = [1 if it is not None and it[0] == "r" else 0 for it in items]
            blocks = [it[1] if o else 0 for it, o in zip(items, ok)]
            chunks = [it[2] if o else 0 for it, o in zip(items, ok)]
            yield (pick(ok) == 1, pick(blocks), pick(chunks), None)

    def for_end(q):
        return (mid,) + end_chunk(q) + (q,)

    def part_for_end(q, first, last):
        @pl.when(mid)
        def _():
            product(*end_chunk(q), half_r, 2 * NCH + q, first, last)

    early = {5: [(0, 0, 1), (1, 0, 1)], 6: [(0, 1, 2), (1, 1, 2), (2, 0, 2)],
             7: [(0, 2, 3), (1, 2, 3), (2, 2, 3), (3, 0, 3)]}
    arrive(1)
    for k in range(NCH):
        advance((true, c, k, None))

    @pl.when(c == 0)
    def _():
        for p in range(4):
            half_copy(p, right).start()

    @pl.when(c == 3)
    def _():
        for p in range(4):
            half_copy(p, left).start()

    for t in range(1, 8):
        if t > 1:
            arrive(t)
        for pos in positions(t):
            advance(pos)
        for q, first, last in early.get(t, []):
            part_for_end(q, first, last)
    arrive(8, "h")
    for q in range(4):
        advance(for_end(q), 3)
    arrive(8, "r")
    advance(for_end(4))
    for pos in positions(8):
        advance(pos)
    for _ in range(6):
        advance(None)

    for i, keeper, got in ((0, 1, res_left), (3, 0, res_right)):
        @pl.when(jnp.logical_and(c == i, r == keeper))
        def _():
            for q in range(NREM):
                b, k = FOR_END[q]
                got(q).wait_recv()
                out_copy(unit_of(b if i == 0 else 3 - b, k)).start()

    for unit in range(2 * NCH):
        out_copy(unit).wait()
    give_sig.wait_send()

    @pl.when(c > 0)
    def _():
        env_left(c).wait_send()

    @pl.when(c < 3)
    def _():
        env_right(c).wait_send()
    for d in range(1, 4):
        @pl.when(c >= d)
        def _(b=c - d):
            @pl.when(c < 3)
            def _():
                env_right(b).wait_send()
            env_x(b).wait_send()
            env_y(b).wait_send()

        @pl.when(c + d <= 3)
        def _(b=c + d):
            @pl.when(c > 0)
            def _():
                env_left(b).wait_send()
            env_x(b).wait_send()
            env_y(b).wait_send()
    for i in range(4):
        @pl.when(c == i)
        def _():
            for first, passed, send in ((FIRST_LEFT, PASS_LEFT, send_left), (FIRST_RIGHT, PASS_RIGHT, send_right)):
                todo = list(first.get(i, []))
                for (j, t), v in passed.items():
                    if j == i:
                        todo += v
                for b, k in todo:
                    send(b, k).wait_send()
            if i in (0, 3):
                for p in range(4):
                    half_copy(p, right if i == 0 else left).wait_send()
    for pos in line:
        if pos is None:
            continue
        valid, b, k, q = pos

        @pl.when(valid)
        def _():
            unit = unit_at(pos)

            @pl.when(b // 2 != r)
            def _():
                row_copy(unit).wait_send()

            @pl.when(b // 2 == r)
            def _():
                x_copy(unit).wait_send()
                y_copy(unit).wait_send()
                if q is not None:
                    @pl.when(c == 1)
                    def _():
                        res_left(q).wait_send()

                    @pl.when(c == 2)
                    def _():
                        res_right(q).wait_send()


def fused(rho_sites, sigma_sites, environment):
    _, pairs, rows, cols = rho_sites.shape
    width = cols // NCH
    units = 2 * NCH + NREM
    sem = pltpu.SemaphoreType.DMA
    piece = (units, width, cols)
    return pl.pallas_call(
        kernel,
        out_shape=jax.ShapeDtypeStruct(environment.shape, F32),
        in_specs=[pl.BlockSpec(memory_space=pl.ANY)] * 3,
        out_specs=pl.BlockSpec(memory_space=pl.ANY),
        scratch_shapes=[
            pltpu.VMEM((4, NCH, pairs, rows, width), BF16),
            pltpu.VMEM((pairs, 2 * rows, cols), BF16),
            pltpu.VMEM((rows, cols), F32),
            pltpu.VMEM((4, rows, cols), BF16),
            pltpu.VMEM((pairs, rows, cols), BF16),
            pltpu.VMEM((pairs, rows, cols), BF16),
            pltpu.VMEM((units + 1, width, cols), F32),
            pltpu.VMEM(piece, BF16), pltpu.VMEM(piece, BF16), pltpu.VMEM(piece, BF16),
            pltpu.VMEM(piece, BF16), pltpu.VMEM(piece, BF16), pltpu.VMEM(piece, BF16),
            pltpu.VMEM(piece, F32),
            sem((4, NCH)), sem((4, NCH)), sem((4, NCH)), sem((4,)), sem((4,)),
            sem((2 + NCH,)), sem, sem,
            sem((4,)), sem((4,)), sem((4,)), sem((4,)), sem((4,)), sem((4,)), sem((4,)),
            sem((units,)), sem((units,)), sem((units,)), sem((units,)), sem((units,)), sem((units,)),
            sem((units,)), sem((NREM,)), sem((NREM,)),
        ],
        compiler_params=pltpu.CompilerParams(
            collective_id=0, has_side_effects=True, vmem_limit_bytes=64 * 1024 * 1024 - 65536
        ),
    )(rho_sites, sigma_sites, environment)


def plain(rho_sites, sigma_sites, environment):
    env_whole = lax.all_gather(environment.astype(BF16), "col", axis=1, tiled=True)
    half = jnp.einsum(
        "ik,pkl->pil",
        env_whole,
        lax.all_gather(sigma_sites[0], "row", axis=1, tiled=True),
        preferred_element_type=F32,
    ).astype(BF16)
    partial_env = jnp.einsum(
        "pij,pil->jl",
        lax.all_gather(rho_sites[0], "col", axis=2, tiled=True),
        half,
        preferred_element_type=F32,
    )
    row_part = lax.psum_scatter(partial_env, "row", scatter_dimension=0, tiled=True)
    return lax.psum(row_part, "phys")


def solution(mesh):
    placed = (P(None, "phys", "row", "col"), P(None, "phys", "row", "col"), P("row", "col"))
    sizes = (mesh.shape["phys"], mesh.shape["row"], mesh.shape["col"])
    body = fused if sizes == (4, 2, 4) else plain
    return jax.shard_map(body, mesh=mesh, in_specs=placed, out_specs=P("row", "col"), check_vma=False)
```
